32 devices in a mesh: trial: 2 (over y), fsdp: 8 (over z, x), tensor: 2 (over core).
Axes of the slice: x: 2, y: 2, z: 4, core: 2. Of those that a mesh axis runs over, the one named last changes fastest.
Arguments:
- tokens: bfloat16 [4096, 4096], P(('trial', 'fsdp'), 'tensor'), parts along dimension 0, may hold values from -110 to 110
- norm_gain: float32 [4096], replicated, may hold values from 0.25 to 1.75
- grow_width: bfloat16 [4096, 2048], P('fsdp'), may hold values from -0.09375 to 0.09375
- old_value: bfloat16 [2048, 1024], P('fsdp', 'tensor'), may hold values from -0.125 to 0.125
- grow_head: bfloat16 [2048, 1024], P('tensor', 'fsdp'), may hold values from -0.1875 to 0.1875
- cotangent: bfloat16 [4096, 2048], P(('trial', 'fsdp'), 'tensor'), parts along dimension 0, may hold values from -6 to 6
Outputs:
- grown_value: bfloat16 [8192, 1024], P(('trial', 'fsdp'), 'tensor'), parts along dimension 0
- value_out: bfloat16 [4096, 2048], P(('trial', 'fsdp'), 'tensor'), parts along dimension 0
- head_grad: float32 [2048, 2048], P(('trial', 'fsdp'), 'tensor'), parts along dimension 0
The draws below stay inside these ranges and needn't reach their ends.
There are 2 independent parts, one for each index of `trial`. The reference program is written for one: setup_inputs(seed, part) draws one part's arguments, and reference() takes and returns one part's arrays. A program takes and returns all parts, laid end to end along the dimension named above; an argument that names none is the same for every part. Nothing has to cross between parts.
All inputs are finite; a program needn't handle non-finite values.
Results may differ from the reference program's by a relative error of at most 0.0064.
Values may be sent and summed in bfloat16 or wider, within the bound.
A program may use at most 64 MiB of HBM per device.

```python
import math
import jax
import jax.numpy as jnp
from jax import lax

D = 4096
DOLD = 2048
HNEW = 2048
HOLD = 1024
TOKENS = 2048


def draw_tokens(key, part):
    base_key = jax.random.fold_in(key, 11)
    first, second, third = jax.random.split(base_key, 3)
    values = jnp.clip(jax.random.normal(first, (TOKENS, D), jnp.float32), -4.0, 4.0)
    top = math.log(10.0)
    row_scale = jnp.exp(jax.random.uniform(second, (TOKENS, 1), jnp.float32, 0.0, top))
    col_scale = jnp.exp(jax.random.uniform(third, (1, D), jnp.float32, 0.0, top))
    return (values * row_scale * col_scale * 0.25).astype(jnp.bfloat16)


def levels(stream_key, dims, shards, least, largest):
    level = 1.0
    for position, parts in shards:
        heights = jax.random.uniform(jax.random.fold_in(jax.random.fold_in(stream_key, 6), position), (parts,), jnp.float32, least / len(shards), largest / len(shards))
        level = level * jnp.repeat(jnp.exp(heights), dims[position] // parts).reshape((-1,) + (1,) * (len(dims) - 1 - position))
    return level


def noise(rng, dims, spread, most, cuts=(), kind=jnp.bfloat16):
    values = jax.random.normal(rng, dims, jnp.float32) * spread
    if len(cuts) > 0:
        values = levels(rng, dims, cuts, -0.22, 0.18) * values
    return jnp.clip(values, min=-most, max=most).astype(kind)


def setup_inputs(seed: int = 0, part: int = 0) -> dict:
    key_list = jax.random.split(jax.random.key(seed), 7)
    own_keys = jax.random.split(jax.random.fold_in(key_list[6], part), 7)
    tokens = draw_tokens(jax.random.fold_in(jax.random.fold_in(key_list[6], part), 71), part)
    norm_gain = jnp.clip(1.0 + 0.15 * jax.random.normal(key_list[1], (D,), jnp.float32), 0.25, 1.75)
    grow_width = noise(key_list[2], (D, DOLD), D ** -0.5, 0.09375, ((0, 8),))
    old_value = noise(key_list[3], (DOLD, HOLD), DOLD ** -0.5, 0.125, ((0, 8), (1, 2)))
    grow_head = noise(key_list[4], (HNEW, HOLD), HOLD ** -0.5, 0.1875, ((0, 2), (1, 8)))
    cotangent = noise(own_keys[5], (TOKENS, HNEW), 1.0, 6.0, ((0, 8), (1, 2)))
    return dict(tokens=tokens, norm_gain=norm_gain, grow_width=grow_width, old_value=old_value, grow_head=grow_head, cotangent=cotangent)


def reference(tokens, norm_gain, grow_width, old_value, grow_head, cotangent):
    widened = tokens.astype(jnp.float32)
    meansq = lax.optimization_barrier(jnp.mean(widened * widened, axis=-1, keepdims=True))
    normed = (widened * jax.lax.rsqrt(meansq + 1e-05) * norm_gain).astype(jnp.bfloat16)
    grown_value = jnp.dot(grow_width, old_value, preferred_element_type=jnp.float32).astype(jnp.bfloat16)
    mixed = jnp.dot(normed, grown_value, preferred_element_type=jnp.float32).astype(jnp.bfloat16)
    value_out = jnp.dot(mixed, grow_head.T, preferred_element_type=jnp.float32).astype(jnp.bfloat16)
    head_grad = jnp.dot(mixed.T, cotangent, preferred_element_type=jnp.float32) * (1.0 / math.sqrt(TOKENS))
    return (grown_value, value_out, head_grad)
```

```python
import math

import jax
import jax.numpy as jnp
from jax import lax
from jax.sharding import PartitionSpec as P


def per_device(tokens, norm_gain, grow_width, old_value, grow_head, cotangent):
    shards = lax.axis_size("fsdp")
    old_half = lax.all_gather(old_value, "fsdp", axis=0, tiled=True)
    grown_value = jnp.dot(grow_width, old_half, preferred_element_type=jnp.float32).astype(
        jnp.bfloat16
    )
    grown_half = lax.all_gather(grown_value, "fsdp", axis=0, tiled=True)
    whole = lax.all_gather(tokens, "tensor", axis=1, tiled=True)
    widened = whole.astype(jnp.float32)
    meansq = jnp.mean(widened * widened, axis=-1, keepdims=True)
    normed = (widened * lax.rsqrt(meansq + 1e-05) * norm_gain).astype(jnp.bfloat16)
    mixed_half = jnp.dot(normed, grown_half, preferred_element_type=jnp.float32).astype(
        jnp.bfloat16
    )
    mixed = lax.all_gather(mixed_half, "tensor", axis=1, tiled=True)
    head_all = lax.all_gather(grow_head, "fsdp", axis=1, tiled=True)
    value_out = lax.dot_general(
        mixed, head_all, (((1,), (1,)), ((), ())), preferred_element_type=jnp.float32
    ).astype(jnp.bfloat16)
    partial = lax.dot_general(
        mixed, cotangent, (((0,), (0,)), ((), ())), preferred_element_type=jnp.float32
    ).astype(jnp.bfloat16)
    partial = partial.reshape(shards, partial.shape[0] // shards, partial.shape[1])
    parts = lax.all_to_all(partial, "fsdp", split_axis=0, concat_axis=0, tiled=True)
    summed = jnp.sum(parts.astype(jnp.float32), axis=0)
    head_grad = summed * (1.0 / math.sqrt(tokens.shape[0] * shards))
    return (grown_value, value_out, head_grad)


def solution(mesh):
    return jax.shard_map(
        per_device,
        mesh=mesh,
        in_specs=(
            P(("trial", "fsdp"), "tensor"),
            P(),
            P("fsdp", None),
            P("fsdp", "tensor"),
            P("tensor", "fsdp"),
            P(("trial", "fsdp"), "tensor"),
        ),
        out_specs=(
            P(("trial", "fsdp"), "tensor"),
            P(("trial", "fsdp"), "tensor"),
            P(("trial", "fsdp"), "tensor"),
        ),
        check_vma=False,
    )
```

```python
import functools
import math

import jax
import jax.numpy as jnp
from jax import lax
from jax.experimental import pallas as pl
from jax.experimental.pallas import tpu as pltpu
from jax.sharding import PartitionSpec as P

MESH = pl.DeviceIdType.MESH
BF16, F32 = jnp.bfloat16, jnp.float32


class Gather:
    def __init__(self, place, buf, sems):
        self.place, self.buf = place, buf
        self.rin, self.ryn, self.sup, self.sdn, self.sx, self.sy = sems
        n, rows, _ = buf.shape
        self.n, self.split = n, rows % 128 == 0
        y = place["y"]
        if self.split:
            self.own_rows = pl.ds(pl.multiple_of(y * (3 * rows // 8), 16), 5 * rows // 8)
            self.y_out = pl.ds(pl.multiple_of(y * (5 * rows // 8), 16), 3 * rows // 8)
            self.y_in = pl.ds(pl.multiple_of((1 - y) * (5 * rows // 8), 16), 3 * rows // 8)
        else:
            self.own_rows = pl.ds(0, rows)

    def copy(self, slot, rows, send, recv, device):
        ref = self.buf.at[slot, rows, :]
        return pltpu.make_async_remote_copy(
            src_ref=ref, dst_ref=ref, send_sem=send, recv_sem=recv,
            device_id=device, device_id_type=MESH,
        )

    def up(self, k):
        p, slot = self.place, k * 2 + self.place["x"]
        return self.copy(slot, self.own_rows, self.sup.at[k], self.rin.at[slot], p["dev"](p["z"] + 1, p["x"]))

    def down(self, k):
        p, slot = self.place, k * 2 + self.place["x"]
        return self.copy(slot, self.own_rows, self.sdn.at[k], self.rin.at[slot], p["dev"](p["z"] - 1, p["x"]))

    def across(self, k):
        p, slot = self.place, k * 2 + self.place["x"]
        return self.copy(slot, self.own_rows, self.sx.at[k], self.rin.at[slot], p["dev"](p["z"], 1 - p["x"]))

    def plane(self, slot, rows):
        p = self.place
        return self.copy(slot, rows, self.sy.at[slot], self.ryn.at[slot], (1 - p["y"], p["g"], p["c"]))

    def arrived(self, slot):
        p = self.place
        self.copy(slot, self.own_rows, self.sx.at[0], self.rin.at[slot], p["dev"](p["z"], 1 - p["x"])).wait_recv()
        if self.split:
            self.plane(slot, self.y_out).start()

    def start(self):
        p = self.place
        z, nz = p["z"], p["nz"]

        @pl.when(z < nz - 1)
        def _():
            self.up(z).start()

        @pl.when(z > 0)
        def _():
            self.down(z).start()

        self.across(z).start()

    def run(self):
        p = self.place
        z, nz, x = p["z"], p["nz"], p["x"]

        def step(s, carry):
            @pl.when(jnp.logical_and(s < nz, z - s >= 0))
            def _():
                self.copy((z - s) * 2 + x, self.own_rows, self.sx.at[0], self.rin.at[(z - s) * 2 + x], p["dev"](z, 1 - x)).wait_recv()

                @pl.when(z < nz - 1)
                def _():
                    self.up(z - s).start()

                self.across(z - s).start()
                if self.split:
                    self.plane((z - s) * 2 + x, self.y_out).start()

            @pl.when(z + s < nz)
            def _():
                self.copy((z + s) * 2 + x, self.own_rows, self.sx.at[0], self.rin.at[(z + s) * 2 + x], p["dev"](z, 1 - x)).wait_recv()

                @pl.when(z > 0)
                def _():
                    self.down(z + s).start()

                self.across(z + s).start()
                if self.split:
                    self.plane((z + s) * 2 + x, self.y_out).start()

            @pl.when(z - (s - 1) >= 0)
            def _():
                self.arrived((z - (s - 1)) * 2 + 1 - x)

            @pl.when(jnp.logical_and(s > 1, z + (s - 1) < nz))
            def _():
                self.arrived((z + (s - 1)) * 2 + 1 - x)

            return carry

        lax.fori_loop(1, nz + 1, step, 0)
        if self.split:
            def take(slot, carry):
                @pl.when(slot != p["g"])
                def _():
                    self.plane(slot, self.y_in).wait_recv()
                return carry

            lax.fori_loop(0, self.n, take, 0)

    def drain(self):
        p = self.place
        z, nz = p["z"], p["nz"]

        def step(k, carry):
            @pl.when(jnp.logical_and(k <= z, z < nz - 1))
            def _():
                self.up(k).wait_send()

            @pl.when(jnp.logical_and(k >= z, z > 0))
            def _():
                self.down(k).wait_send()

            self.across(k).wait_send()
            return carry

        lax.fori_loop(0, nz, step, 0)
        if self.split:
            def sent(slot, carry):
                @pl.when(slot != p["g"])
                def _():
                    self.plane(slot, self.y_out).wait_send()
                return carry

            lax.fori_loop(0, self.n, sent, 0)


def kernel(n, inside, scale, *refs):
    it = iter(refs)
    tok_in, gain, width_in, old_in, head_in, cot_in = (next(it) for _ in range(6))
    grown_out = next(it)
    if inside:
        value_out, grad_out = next(it), next(it)
    else:
        mixed_out = next(it)
    tok, width, normed, mixed, oldb, grownb = (next(it) for _ in range(6))
    old_sems = [next(it) for _ in range(6)]
    grown_sems = [next(it) for _ in range(6)]
    local, pair_s, pair_r = next(it), next(it), next(it)
    if inside:
        headb, cot, tx, rx, tz, rz, own = (next(it) for _ in range(7))
        head_sems = [next(it) for _ in range(6)]
        xs, xr, zs, zr = (next(it) for _ in range(4))

    y, g, c = lax.axis_index("trial"), lax.axis_index("fsdp"), lax.axis_index("tensor")
    nz = n // 2
    z, x = g // 2, g % 2

    def dev(zz, xx):
        return (y, zz * 2 + xx, c)

    place = dict(y=y, g=g, c=c, z=z, x=x, nz=nz, dev=dev)

    loads = [
        pltpu.make_async_copy(old_in, oldb.at[g], local.at[0]),
        pltpu.make_async_copy(tok_in, tok.at[c], local.at[1]),
        pltpu.make_async_copy(width_in, width, local.at[2]),
    ]
    if inside:
        loads.append(pltpu.make_async_copy(head_in, headb.at[g], local.at[3]))
        loads.append(pltpu.make_async_copy(cot_in, cot, local.at[4]))
    for load in loads:
        load.start()

    barrier = pltpu.get_barrier_semaphore()

    def greet(k, carry):
        @pl.when(k != z)
        def _():
            pl.semaphore_signal(barrier, inc=1, device_id=dev(k, x), device_id_type=MESH)
        return carry

    lax.fori_loop(0, nz, greet, 0)
    core = (y, g, 1 - c)
    for other in (dev(z, 1 - x), (1 - y, g, c), core):
        pl.semaphore_signal(barrier, inc=1, device_id=other, device_id_type=MESH)
    pl.semaphore_wait(barrier, nz - 1 + 3)

    old = Gather(place, oldb, old_sems)
    grown = Gather(place, grownb, grown_sems)
    loads[0].wait()
    old.start()
    loads[1].wait()
    swap = pltpu.make_async_remote_copy(
        src_ref=tok.at[c], dst_ref=tok.at[c], send_sem=pair_s.at[0], recv_sem=pair_r.at[0],
        device_id=core, device_id_type=MESH,
    )
    swap.start()
    swap.wait()

    count, half_d = tok.shape[1], tok.shape[2]

    @pl.loop(0, count // 16)
    def _(i):
        rows = pl.ds(pl.multiple_of(i * 16, 16), 16)
        a, b = tok[0, rows, :].astype(F32), tok[1, rows, :].astype(F32)
        total = jnp.sum(a * a, axis=-1, keepdims=True) + jnp.sum(b * b, axis=-1, keepdims=True)
        inv = lax.rsqrt(total * (1.0 / (2 * half_d)) + 1e-05)
        normed[rows, pl.ds(0, half_d)] = (a * inv * gain[:, pl.ds(0, half_d)]).astype(BF16)
        normed[rows, pl.ds(half_d, half_d)] = (b * inv * gain[:, pl.ds(half_d, half_d)]).astype(BF16)

    old.run()
    if inside:
        head = Gather(place, headb, head_sems)
        loads[3].wait()
        head.start()
    loads[2].wait()
    feats = oldb.shape[2]

    @pl.loop(0, feats // 256)
    def _(j):
        cols = pl.ds(pl.multiple_of(j * 256, 256), 256)
        rhs = oldb[:, :, cols].reshape(-1, 256)
        grownb[g, :, cols] = jnp.dot(width[...], rhs, preferred_element_type=F32).astype(BF16)

    grown.start()
    grown_out[...] = grownb[g]
    grown.run()

    @pl.loop(0, feats // 256)
    def _(j):
        cols = pl.ds(pl.multiple_of(j * 256, 256), 256)
        rhs = grownb[:, :, cols].reshape(-1, 256)
        mixed[c, :, cols] = jnp.dot(normed[...], rhs, preferred_element_type=F32).astype(BF16)

    share = pltpu.make_async_remote_copy(
        src_ref=mixed.at[c], dst_ref=mixed.at[c], send_sem=pair_s.at[1], recv_sem=pair_r.at[1],
        device_id=core, device_id_type=MESH,
    )
    share.start()
    share.wait()

    if inside:
        w = headb.shape[2]
        per_half = n // 2
        loads[4].wait()

        def block(slot):
            cols = pl.ds(pl.multiple_of((slot % per_half) * w, w), w)
            return mixed[slot // per_half, :, cols]

        def partial(slot):
            return lax.dot_general(
                block(slot), cot[...], (((0,), (0,)), ((), ())), preferred_element_type=F32
            )

        def hop(k):
            return pltpu.make_async_remote_copy(
                src_ref=tx.at[k], dst_ref=rx.at[k], send_sem=xs.at[k], recv_sem=xr.at[k],
                device_id=dev(z, 1 - x), device_id_type=MESH,
            )

        def deliver(k):
            return pltpu.make_async_remote_copy(
                src_ref=tz.at[k], dst_ref=rz.at[z], send_sem=zs.at[k], recv_sem=zr.at[z],
                device_id=dev(k, x), device_id_type=MESH,
            )

        def receive(k):
            return pltpu.make_async_remote_copy(
                src_ref=tz.at[k], dst_ref=rz.at[k], send_sem=zs.at[k], recv_sem=zr.at[k],
                device_id=dev(k, x), device_id_type=MESH,
            )

        def first(i, carry):
            k = (z + 1 + i) % nz
            tx[k] = partial(k * 2 + 1 - x).astype(BF16)
            hop(k).start()
            return carry

        lax.fori_loop(0, nz, first, 0)
        head.run()

        def second(i, carry):
            k = (z + 1 + i) % nz
            mine = partial(k * 2 + x)
            hop(k).wait_recv()
            mine = mine + rx[k].astype(F32)

            @pl.when(k != z)
            def _():
                tz[k] = mine.astype(BF16)
                deliver(k).start()

            @pl.when(k == z)
            def _():
                own[...] = mine
            return carry

        lax.fori_loop(0, nz, second, 0)

        @pl.loop(0, value_out.shape[1] // 256)
        def _(j):
            outs = pl.ds(pl.multiple_of(j * 256, 256), 256)
            total = jnp.zeros((count, 256), F32)
            for slot in range(n):
                lhs = mixed[slot // per_half, :, pl.ds((slot % per_half) * w, w)]
                total = total + lax.dot_general(
                    lhs, headb[slot, outs, :], (((1,), (1,)), ((), ())), preferred_element_type=F32
                )
            value_out[:, outs] = total.astype(BF16)

        def collect(k, carry):
            @pl.when(k != z)
            def _():
                receive(k).wait_recv()
                own[...] += rz[k].astype(F32)
            return carry

        lax.fori_loop(0, nz, collect, 0)
        grad_out[...] = own[...] * scale

        def sent(k, carry):
            hop(k).wait_send()

            @pl.when(k != z)
            def _():
                deliver(k).wait_send()
            return carry

        lax.fori_loop(0, nz, sent, 0)
        head.drain()
    else:
        mixed_out[...] = mixed[...]
    old.drain()
    grown.drain()


def gather_sems(n):
    dma = pltpu.SemaphoreType.DMA
    return [dma((n,)), dma((n,)), dma((n // 2,)), dma((n // 2,)), dma((n // 2,)), dma((n,))]


def per_device(tokens, norm_gain, grow_width, old_value, grow_head, cotangent):
    n = lax.axis_size("fsdp")
    count, half_d = tokens.shape
    feats = old_value.shape[1]
    slab = grow_width.shape[0]
    heads, w = grow_head.shape
    inside = w % 128 == 0
    scale = 1.0 / math.sqrt(count * n)
    dma = pltpu.SemaphoreType.DMA
    vm = pl.BlockSpec(memory_space=pltpu.VMEM)
    hbm = pl.BlockSpec(memory_space=pl.ANY)
    outs = [jax.ShapeDtypeStruct((slab, feats), BF16)]
    if inside:
        outs += [jax.ShapeDtypeStruct((count, heads), BF16), jax.ShapeDtypeStruct((w, heads), F32)]
    else:
        outs += [jax.ShapeDtypeStruct((2, count, feats), BF16)]
    scratch = [
        pltpu.VMEM((2, count, half_d), BF16),
        pltpu.VMEM(grow_width.shape, BF16),
        pltpu.VMEM((count, 2 * half_d), BF16),
        pltpu.VMEM((2, count, feats), BF16),
        pltpu.VMEM((n,) + old_value.shape, BF16),
        pltpu.VMEM((n, slab, feats), BF16),
        *gather_sems(n), *gather_sems(n),
        dma((5,)), dma((2,)), dma((2,)),
    ]
    if inside:
        piece = pltpu.VMEM((n // 2, w, heads), BF16)
        scratch += [
            pltpu.VMEM((n, heads, w), BF16), pltpu.VMEM((count, heads), BF16),
            piece, piece, piece, piece, pltpu.VMEM((w, heads), F32),
            *gather_sems(n),
            dma((n // 2,)), dma((n // 2,)), dma((n // 2,)), dma((n // 2,)),
        ]
    results = pl.pallas_call(
        functools.partial(kernel, n, inside, scale),
        out_shape=outs,
        in_specs=[hbm, vm, hbm, hbm, hbm, hbm],
        out_specs=[vm] * len(outs),
        scratch_shapes=scratch,
        compiler_params=pltpu.CompilerParams(
            collective_id=0, has_side_effects=True, vmem_limit_bytes=48 * 1024 * 1024
        ),
    )(tokens, norm_gain.reshape(1, -1), grow_width, old_value, grow_head, cotangent)
    if inside:
        return tuple(results)
    grown_value, halves = results
    mixed = jnp.concatenate([halves[0], halves[1]], axis=1)
    head_all = lax.all_gather(grow_head, "fsdp", axis=1, tiled=True)
    value_out = lax.dot_general(
        mixed, head_all, (((1,), (1,)), ((), ())), preferred_element_type=F32
    ).astype(BF16)
    partial = lax.dot_general(
        mixed, cotangent, (((0,), (0,)), ((), ())), preferred_element_type=F32
    ).astype(BF16)
    partial = partial.reshape(n, partial.shape[0] // n, partial.shape[1])
    parts = lax.all_to_all(partial, "fsdp", split_axis=0, concat_axis=0, tiled=True)
    return (grown_value, value_out, jnp.sum(parts.astype(F32), axis=0) * scale)


def solution(mesh):
    return jax.shard_map(
        per_device,
        mesh=mesh,
        in_specs=(
            P(("trial", "fsdp"), "tensor"),
            P(),
            P("fsdp", None),
            P("fsdp", "tensor"),
            P("tensor", "fsdp"),
            P(("trial", "fsdp"), "tensor"),
        ),
        out_specs=(
            P(("trial", "fsdp"), "tensor"),
            P(("trial", "fsdp"), "tensor"),
            P(("trial", "fsdp"), "tensor"),
        ),
        check_vma=False,
    )
```

```python
import functools
import math

import jax
import jax.numpy as jnp
from jax import lax
from jax.experimental import pallas as pl
from jax.experimental.pallas import tpu as pltpu
from jax.sharding import PartitionSpec as P

MESH = pl.DeviceIdType.MESH
BF16, F32 = jnp.bfloat16, jnp.float32


class Gather:
    def __init__(self, place, buf, sems):
        self.place, self.buf = place, buf
        self.rin, self.ryn, self.sup, self.sdn, self.sx, self.sy = sems
        n, rows, _ = buf.shape
        self.n, self.split = n, rows % 128 == 0
        y = place["y"]
        if self.split:
            self.own_rows = pl.ds(pl.multiple_of(y * (3 * rows // 8), 16), 5 * rows // 8)
            self.y_out = pl.ds(pl.multiple_of(y * (5 * rows // 8), 16), 3 * rows // 8)
            self.y_in = pl.ds(pl.multiple_of((1 - y) * (5 * rows // 8), 16), 3 * rows // 8)
        else:
            self.own_rows = pl.ds(0, rows)

    def copy(self, slot, rows, send, recv, device):
        ref = self.buf.at[slot, rows, :]
        return pltpu.make_async_remote_copy(
            src_ref=ref, dst_ref=ref, send_sem=send, recv_sem=recv,
            device_id=device, device_id_type=MESH,
        )

    def up(self, k):
        p, slot = self.place, k * 2 + self.place["x"]
        return self.copy(slot, self.own_rows, self.sup.at[k], self.rin.at[slot], p["dev"](p["z"] + 1, p["x"]))

    def down(self, k):
        p, slot = self.place, k * 2 + self.place["x"]
        return self.copy(slot, self.own_rows, self.sdn.at[k], self.rin.at[slot], p["dev"](p["z"] - 1, p["x"]))

    def across(self, k):
        p, slot = self.place, k * 2 + self.place["x"]
        return self.copy(slot, self.own_rows, self.sx.at[k], self.rin.at[slot], p["dev"](p["z"], 1 - p["x"]))

    def plane(self, slot, rows):
        p = self.place
        return self.copy(slot, rows, self.sy.at[slot], self.ryn.at[slot], (1 - p["y"], p["g"], p["c"]))

    def arrived(self, slot):
        p = self.place
        self.copy(slot, self.own_rows, self.sx.at[0], self.rin.at[slot], p["dev"](p["z"], 1 - p["x"])).wait_recv()
        if self.split:
            self.plane(slot, self.y_out).start()

    def start(self):
        p = self.place
        z, nz = p["z"], p["nz"]

        @pl.when(z < nz - 1)
        def _():
            self.up(z).start()

        @pl.when(z > 0)
        def _():
            self.down(z).start()

        self.across(z).start()

    def step(self, s):
        p = self.place
        z, nz, x = p["z"], p["nz"], p["x"]
        @pl.when(jnp.logical_and(s < nz, z - s >= 0))
        def _():
            self.copy((z - s) * 2 + x, self.own_rows, self.sx.at[0], self.rin.at[(z - s) * 2 + x], p["dev"](z, 1 - x)).wait_recv()

            @pl.when(z < nz - 1)
            def _():
                self.up(z - s).start()

            self.across(z - s).start()
            if self.split:
                self.plane((z - s) * 2 + x, self.y_out).start()

        @pl.when(z + s < nz)
        def _():
            self.copy((z + s) * 2 + x, self.own_rows, self.sx.at[0], self.rin.at[(z + s) * 2 + x], p["dev"](z, 1 - x)).wait_recv()

            @pl.when(z > 0)
            def _():
                self.down(z + s).start()

            self.across(z + s).start()
            if self.split:
                self.plane((z + s) * 2 + x, self.y_out).start()

        @pl.when(z - (s - 1) >= 0)
        def _():
            self.arrived((z - (s - 1)) * 2 + 1 - x)

        @pl.when(jnp.logical_and(s > 1, z + (s - 1) < nz))
        def _():
            self.arrived((z + (s - 1)) * 2 + 1 - x)

    def finish(self):
        p = self.place
        if self.split:
            def take(slot, carry):
                @pl.when(slot != p["g"])
                def _():
                    self.plane(slot, self.y_in).wait_recv()
                return carry

            lax.fori_loop(0, self.n, take, 0)

    def drain(self):
        p = self.place
        z, nz = p["z"], p["nz"]

        def step(k, carry):
            @pl.when(jnp.logical_and(k <= z, z < nz - 1))
            def _():
                self.up(k).wait_send()

            @pl.when(jnp.logical_and(k >= z, z > 0))
            def _():
                self.down(k).wait_send()

            self.across(k).wait_send()
            return carry

        lax.fori_loop(0, nz, step, 0)
        if self.split:
            def sent(slot, carry):
                @pl.when(slot != p["g"])
                def _():
                    self.plane(slot, self.y_out).wait_send()
                return carry

            lax.fori_loop(0, self.n, sent, 0)


def kernel(n, inside, scale, *refs):
    it = iter(refs)
    tok_in, gain, width_in, old_in, head_in, cot_in = (next(it) for _ in range(6))
    grown_out = next(it)
    if inside:
        value_out, grad_out = next(it), next(it)
    else:
        mixed_out = next(it)
    tok, width, normed, mixed, oldb, grownb = (next(it) for _ in range(6))
    old_sems = [next(it) for _ in range(6)]
    grown_sems = [next(it) for _ in range(6)]
    local, pair_s, pair_r = next(it), next(it), next(it)
    if inside:
        headb, cot, theirs, tz, ru, rd, own = (next(it) for _ in range(7))
        head_sems = [next(it) for _ in range(6)]
        xs, xr, zs, ur, dr = (next(it) for _ in range(5))

    y, g, c = lax.axis_index("trial"), lax.axis_index("fsdp"), lax.axis_index("tensor")
    nz = n // 2
    z, x = g // 2, g % 2

    def dev(zz, xx):
        return (y, zz * 2 + xx, c)

    place = dict(y=y, g=g, c=c, z=z, x=x, nz=nz, dev=dev)

    loads = [
        pltpu.make_async_copy(old_in, oldb.at[g], local.at[0]),
        pltpu.make_async_copy(tok_in, tok.at[c], local.at[1]),
        pltpu.make_async_copy(width_in, width, local.at[2]),
    ]
    if inside:
        loads.append(pltpu.make_async_copy(head_in, headb.at[g], local.at[3]))
        loads.append(pltpu.make_async_copy(cot_in, cot.at[0], local.at[4]))
    for load in loads:
        load.start()

    barrier = pltpu.get_barrier_semaphore()

    def greet(k, carry):
        @pl.when(k != z)
        def _():
            pl.semaphore_signal(barrier, inc=1, device_id=dev(k, x), device_id_type=MESH)
        return carry

    lax.fori_loop(0, nz, greet, 0)
    core = (y, g, 1 - c)
    for other in (dev(z, 1 - x), (1 - y, g, c), core):
        pl.semaphore_signal(barrier, inc=1, device_id=other, device_id_type=MESH)
    pl.semaphore_wait(barrier, nz - 1 + 3)

    old = Gather(place, oldb, old_sems)
    grown = Gather(place, grownb, grown_sems)
    loads[0].wait()
    old.start()
    loads[1].wait()
    swap = pltpu.make_async_remote_copy(
        src_ref=tok.at[c], dst_ref=tok.at[c], send_sem=pair_s.at[0], recv_sem=pair_r.at[0],
        device_id=core, device_id_type=MESH,
    )
    swap.start()
    count, half_d = tok.shape[1], tok.shape[2]

    def walk_old(s, carry):
        old.step(s)
        return carry

    lax.fori_loop(1, nz + 1, walk_old, 0)
    old.finish()
    if inside:
        head = Gather(place, headb, head_sems)
        loads[3].wait()
        head.start()
        loads[4].wait()
        lend = pltpu.make_async_remote_copy(
            src_ref=cot.at[0], dst_ref=cot.at[1], send_sem=pair_s.at[2], recv_sem=pair_r.at[2],
            device_id=dev(z, 1 - x), device_id_type=MESH,
        )
        lend.start()
    loads[2].wait()
    feats = oldb.shape[2]

    @pl.loop(0, feats // 256)
    def _(j):
        cols = pl.ds(pl.multiple_of(j * 256, 256), 256)
        rhs = oldb[:, :, cols].reshape(-1, 256)
        grownb[g, :, cols] = jnp.dot(width[...], rhs, preferred_element_type=F32).astype(BF16)

    grown.start()
    grown_out[...] = grownb[g]
    swap.wait()

    @pl.loop(0, count // 16)
    def _(i):
        rows = pl.ds(pl.multiple_of(i * 16, 16), 16)
        a, b = tok[0, rows, :].astype(F32), tok[1, rows, :].astype(F32)
        total = jnp.sum(a * a, axis=-1, keepdims=True) + jnp.sum(b * b, axis=-1, keepdims=True)
        inv = lax.rsqrt(total * (1.0 / (2 * half_d)) + 1e-05)
        normed[rows, pl.ds(0, half_d)] = (a * inv * gain[:, pl.ds(0, half_d)]).astype(BF16)
        normed[rows, pl.ds(half_d, half_d)] = (b * inv * gain[:, pl.ds(half_d, half_d)]).astype(BF16)

    def walk_grown(s, carry):
        if inside:
            head.step(s)
        grown.step(s)
        return carry

    lax.fori_loop(1, nz + 1, walk_grown, 0)
    grown.finish()

    @pl.loop(0, feats // 256)
    def _(j):
        cols = pl.ds(pl.multiple_of(j * 256, 256), 256)
        rhs = grownb[:, :, cols].reshape(-1, 256)
        mixed[c, :, cols] = jnp.dot(normed[...], rhs, preferred_element_type=F32).astype(BF16)

    share = pltpu.make_async_remote_copy(
        src_ref=mixed.at[c], dst_ref=mixed.at[c], send_sem=pair_s.at[1], recv_sem=pair_r.at[1],
        device_id=core, device_id_type=MESH,
    )
    share.start()
    share.wait()

    if inside:
        w = headb.shape[2]
        per_half = n // 2

        def block(slot):
            cols = pl.ds(pl.multiple_of((slot % per_half) * w, w), w)
            return mixed.at[slot // per_half, :, cols]

        def hand(k):
            return pltpu.make_async_remote_copy(
                src_ref=block(k * 2 + 1 - x), dst_ref=theirs.at[k], send_sem=xs.at[k],
                recv_sem=xr.at[k], device_id=dev(z, 1 - x), device_id_type=MESH,
            )

        def offer(i, carry):
            @pl.when(nz - 1 - i > i)
            def _():
                hand(nz - 1 - i).start()

            @pl.when(nz - 1 - i >= i)
            def _():
                hand(i).start()
            return carry

        lax.fori_loop(0, nz, offer, 0)
        lend.wait_recv()

        def partial(k):
            rows = (((0,), (0,)), ((), ()))
            mine = lax.dot_general(block(k * 2 + x)[...], cot[0], rows, preferred_element_type=F32)
            return mine + lax.dot_general(theirs[k], cot[1], rows, preferred_element_type=F32)

        def rise(k):
            return pltpu.make_async_remote_copy(
                src_ref=tz.at[k], dst_ref=ru.at[k], send_sem=zs.at[k], recv_sem=ur.at[k],
                device_id=dev(z + 1, x), device_id_type=MESH,
            )

        def sink(k):
            return pltpu.make_async_remote_copy(
                src_ref=tz.at[k], dst_ref=rd.at[k], send_sem=zs.at[k], recv_sem=dr.at[k],
                device_id=dev(z - 1, x), device_id_type=MESH,
            )

        def mine(k, carry):
            hand(k).wait_recv()
            return carry

        lax.fori_loop(0, nz, mine, 0)

        def chain(i, carry):
            k = nz - 1 - i

            @pl.when(k > z)
            def _():
                own[...] = partial(k)

                @pl.when(z > 0)
                def _():
                    rise(k).wait_recv()
                    own[...] += ru[k].astype(F32)

                tz[k] = own[...].astype(BF16)
                rise(k).start()

            @pl.when(i < z)
            def _():
                own[...] = partial(i)

                @pl.when(z < nz - 1)
                def _():
                    sink(i).wait_recv()
                    own[...] += rd[i].astype(F32)

                tz[i] = own[...].astype(BF16)
                sink(i).start()
            return carry

        lax.fori_loop(0, nz - 1, chain, 0)
        own[...] = partial(z)
        head.finish()

        @pl.loop(0, value_out.shape[1] // 256)
        def _(j):
            outs = pl.ds(pl.multiple_of(j * 256, 256), 256)
            total = jnp.zeros((count, 256), F32)
            for slot in range(n):
                lhs = mixed[slot // per_half, :, pl.ds((slot % per_half) * w, w)]
                total = total + lax.dot_general(
                    lhs, headb[slot, outs, :], (((1,), (1,)), ((), ())), preferred_element_type=F32
                )
            value_out[:, outs] = total.astype(BF16)

        @pl.when(z > 0)
        def _():
            rise(z).wait_recv()
            own[...] += ru[z].astype(F32)

        @pl.when(z < nz - 1)
        def _():
            sink(z).wait_recv()
            own[...] += rd[z].astype(F32)

        grad_out[...] = own[...] * scale
        lend.wait_send()

        def sent(k, carry):
            hand(k).wait_send()

            @pl.when(k > z)
            def _():
                rise(k).wait_send()

            @pl.when(k < z)
            def _():
                sink(k).wait_send()
            return carry

        lax.fori_loop(0, nz, sent, 0)
        head.drain()
    else:
        mixed_out[...] = mixed[...]
    old.drain()
    grown.drain()


def gather_sems(n):
    dma = pltpu.SemaphoreType.DMA
    return [dma((n,)), dma((n,)), dma((n // 2,)), dma((n // 2,)), dma((n // 2,)), dma((n,))]


def per_device(tokens, norm_gain, grow_width, old_value, grow_head, cotangent):
    n = lax.axis_size("fsdp")
    count, half_d = tokens.shape
    feats = old_value.shape[1]
    slab = grow_width.shape[0]
    heads, w = grow_head.shape
    inside = w % 128 == 0
    scale = 1.0 / math.sqrt(count * n)
    dma = pltpu.SemaphoreType.DMA
    vm = pl.BlockSpec(memory_space=pltpu.VMEM)
    hbm = pl.BlockSpec(memory_space=pl.ANY)
    outs = [jax.ShapeDtypeStruct((slab, feats), BF16)]
    if inside:
        outs += [jax.ShapeDtypeStruct((count, heads), BF16), jax.ShapeDtypeStruct((w, heads), F32)]
    else:
        outs += [jax.ShapeDtypeStruct((2, count, feats), BF16)]
    scratch = [
        pltpu.VMEM((2, count, half_d), BF16),
        pltpu.VMEM(grow_width.shape, BF16),
        pltpu.VMEM((count, 2 * half_d), BF16),
        pltpu.VMEM((2, count, feats), BF16),
        pltpu.VMEM((n,) + old_value.shape, BF16),
        pltpu.VMEM((n, slab, feats), BF16),
        *gather_sems(n), *gather_sems(n),
        dma((5,)), dma((3,)), dma((3,)),
    ]
    if inside:
        piece = pltpu.VMEM((n // 2, w, heads), BF16)
        scratch += [
            pltpu.VMEM((n, heads, w), BF16), pltpu.VMEM((2, count, heads), BF16),
            pltpu.VMEM((n // 2, count, w), BF16), piece, piece, piece, pltpu.VMEM((w, heads), F32),
            *gather_sems(n),
            dma((n // 2,)), dma((n // 2,)), dma((n // 2,)), dma((n // 2,)), dma((n // 2,)),
        ]
    results = pl.pallas_call(
        functools.partial(kernel, n, inside, scale),
        out_shape=outs,
        in_specs=[hbm, vm, hbm, hbm, hbm, hbm],
        out_specs=[vm] * len(outs),
        scratch_shapes=scratch,
        compiler_params=pltpu.CompilerParams(
            collective_id=0, has_side_effects=True, vmem_limit_bytes=48 * 1024 * 1024
        ),
    )(tokens, norm_gain.reshape(1, -1), grow_width, old_value, grow_head, cotangent)
    if inside:
        return tuple(results)
    grown_value, halves = results
    mixed = jnp.concatenate([halves[0], halves[1]], axis=1)
    head_all = lax.all_gather(grow_head, "fsdp", axis=1, tiled=True)
    value_out = lax.dot_general(
        mixed, head_all, (((1,), (1,)), ((), ())), preferred_element_type=F32
    ).astype(BF16)
    partial = lax.dot_general(
        mixed, cotangent, (((0,), (0,)), ((), ())), preferred_element_type=F32
    ).astype(BF16)
    partial = partial.reshape(n, partial.shape[0] // n, partial.shape[1])
    parts = lax.all_to_all(partial, "fsdp", split_axis=0, concat_axis=0, tiled=True)
    return (grown_value, value_out, jnp.sum(parts.astype(F32), axis=0) * scale)


def solution(mesh):
    return jax.shard_map(
        per_device,
        mesh=mesh,
        in_specs=(
            P(("trial", "fsdp"), "tensor"),
            P(),
            P("fsdp", None),
            P("fsdp", "tensor"),
            P("tensor", "fsdp"),
            P(("trial", "fsdp"), "tensor"),
        ),
        out_specs=(
            P(("trial", "fsdp"), "tensor"),
            P(("trial", "fsdp"), "tensor"),
            P(("trial", "fsdp"), "tensor"),
        ),
        check_vma=False,
    )
```

```python
import functools
import math

import jax
import jax.numpy as jnp
from jax import lax
from jax.experimental import pallas as pl
from jax.experimental.pallas import tpu as pltpu
from jax.sharding import PartitionSpec as P

MESH = pl.DeviceIdType.MESH
BF16, F32 = jnp.bfloat16, jnp.float32


class Gather:
    def __init__(self, place, buf, sems, part=0, parts=1):
        self.place, self.buf = place, buf
        self.rin, self.ryn, self.sup, self.sdn, self.sx, self.sy = sems
        n, rows = buf.shape[0], buf.shape[1] // parts
        base = part * rows
        self.n, self.split = n, rows % 128 == 0
        y = place["y"]
        if self.split:
            self.own_rows = pl.ds(pl.multiple_of(base + y * (3 * rows // 8), 16), 5 * rows // 8)
            self.y_out = pl.ds(pl.multiple_of(base + y * (5 * rows // 8), 16), 3 * rows // 8)
            self.y_in = pl.ds(pl.multiple_of(base + (1 - y) * (5 * rows // 8), 16), 3 * rows // 8)
        else:
            self.own_rows = pl.ds(base, rows)

    def copy(self, slot, rows, send, recv, device):
        ref = self.buf.at[slot, rows, :]
        return pltpu.make_async_remote_copy(
            src_ref=ref, dst_ref=ref, send_sem=send, recv_sem=recv,
            device_id=device, device_id_type=MESH,
        )

    def up(self, k):
        p, slot = self.place, k * 2 + self.place["x"]
        return self.copy(slot, self.own_rows, self.sup.at[k], self.rin.at[slot], p["dev"](p["z"] + 1, p["x"]))

    def down(self, k):
        p, slot = self.place, k * 2 + self.place["x"]
        return self.copy(slot, self.own_rows, self.sdn.at[k], self.rin.at[slot], p["dev"](p["z"] - 1, p["x"]))

    def across(self, k):
        p, slot = self.place, k * 2 + self.place["x"]
        return self.copy(slot, self.own_rows, self.sx.at[k], self.rin.at[slot], p["dev"](p["z"], 1 - p["x"]))

    def plane(self, slot, rows):
        p = self.place
        return self.copy(slot, rows, self.sy.at[slot], self.ryn.at[slot], (1 - p["y"], p["g"], p["c"]))

    def arrived(self, slot):
        p = self.place
        self.copy(slot, self.own_rows, self.sx.at[0], self.rin.at[slot], p["dev"](p["z"], 1 - p["x"])).wait_recv()
        if self.split:
            self.plane(slot, self.y_out).start()

    def start(self):
        p = self.place
        z, nz = p["z"], p["nz"]

        @pl.when(z < nz - 1)
        def _():
            self.up(z).start()

        @pl.when(z > 0)
        def _():
            self.down(z).start()

        self.across(z).start()

    def step(self, s):
        p = self.place
        z, nz, x = p["z"], p["nz"], p["x"]
        @pl.when(jnp.logical_and(s < nz, z - s >= 0))
        def _():
            self.copy((z - s) * 2 + x, self.own_rows, self.sx.at[0], self.rin.at[(z - s) * 2 + x], p["dev"](z, 1 - x)).wait_recv()

            @pl.when(z < nz - 1)
            def _():
                self.up(z - s).start()

            self.across(z - s).start()
            if self.split:
                self.plane((z - s) * 2 + x, self.y_out).start()

        @pl.when(z + s < nz)
        def _():
            self.copy((z + s) * 2 + x, self.own_rows, self.sx.at[0], self.rin.at[(z + s) * 2 + x], p["dev"](z, 1 - x)).wait_recv()

            @pl.when(z > 0)
            def _():
                self.down(z + s).start()

            self.across(z + s).start()
            if self.split:
                self.plane((z + s) * 2 + x, self.y_out).start()

        @pl.when(z - (s - 1) >= 0)
        def _():
            self.arrived((z - (s - 1)) * 2 + 1 - x)

        @pl.when(jnp.logical_and(s > 1, z + (s - 1) < nz))
        def _():
            self.arrived((z + (s - 1)) * 2 + 1 - x)

    def finish(self):
        p = self.place
        if self.split:
            def take(slot, carry):
                @pl.when(slot != p["g"])
                def _():
                    self.plane(slot, self.y_in).wait_recv()
                return carry

            lax.fori_loop(0, self.n, take, 0)

    def drain(self):
        p = self.place
        z, nz = p["z"], p["nz"]

        def step(k, carry):
            @pl.when(jnp.logical_and(k <= z, z < nz - 1))
            def _():
                self.up(k).wait_send()

            @pl.when(jnp.logical_and(k >= z, z > 0))
            def _():
                self.down(k).wait_send()

            self.across(k).wait_send()
            return carry

        lax.fori_loop(0, nz, step, 0)
        if self.split:
            def sent(slot, carry):
                @pl.when(slot != p["g"])
                def _():
                    self.plane(slot, self.y_out).wait_send()
                return carry

            lax.fori_loop(0, self.n, sent, 0)


def kernel(n, inside, scale, *refs):
    it = iter(refs)
    tok_in, gain, width_in, old_in, head_in, cot_in = (next(it) for _ in range(6))
    grown_out = next(it)
    if inside:
        value_out, grad_out = next(it), next(it)
    else:
        mixed_out = next(it)
    tok, width, normed, mixed, oldb, grownb = (next(it) for _ in range(6))
    old_parts, grown_parts = cuts(oldb.shape[1]), cuts(grownb.shape[1])
    old_sems = [[next(it) for _ in range(6)] for _ in range(old_parts)]
    grown_sems = [[next(it) for _ in range(6)] for _ in range(grown_parts)]
    local, pair_s, pair_r = next(it), next(it), next(it)
    if inside:
        headb, cot, theirs, tz, ru, rd, own = (next(it) for _ in range(7))
        head_sems = [next(it) for _ in range(6)]
        xs, xr, zs, ur, dr = (next(it) for _ in range(5))

    y, g, c = lax.axis_index("trial"), lax.axis_index("fsdp"), lax.axis_index("tensor")
    nz = n // 2
    z, x = g // 2, g % 2

    def dev(zz, xx):
        return (y, zz * 2 + xx, c)

    place = dict(y=y, g=g, c=c, z=z, x=x, nz=nz, dev=dev)

    loads = [
        pltpu.make_async_copy(old_in, oldb.at[g], local.at[0]),
        pltpu.make_async_copy(tok_in, tok.at[c], local.at[1]),
        pltpu.make_async_copy(width_in, width, local.at[2]),
    ]
    if inside:
        loads.append(pltpu.make_async_copy(head_in, headb.at[g], local.at[3]))
        loads.append(pltpu.make_async_copy(cot_in, cot.at[0], local.at[4]))
    for load in loads:
        load.start()

    barrier = pltpu.get_barrier_semaphore()

    def greet(k, carry):
        @pl.when(k != z)
        def _():
            pl.semaphore_signal(barrier, inc=1, device_id=dev(k, x), device_id_type=MESH)
        return carry

    lax.fori_loop(0, nz, greet, 0)
    core = (y, g, 1 - c)
    for other in (dev(z, 1 - x), (1 - y, g, c), core):
        pl.semaphore_signal(barrier, inc=1, device_id=other, device_id_type=MESH)
    pl.semaphore_wait(barrier, nz - 1 + 3)

    old = [Gather(place, oldb, sems, i, old_parts) for i, sems in enumerate(old_sems)]
    grown = [Gather(place, grownb, sems, i, grown_parts) for i, sems in enumerate(grown_sems)]
    loads[0].wait()
    for part in old:
        part.start()
    loads[1].wait()
    swap = pltpu.make_async_remote_copy(
        src_ref=tok.at[c], dst_ref=tok.at[c], send_sem=pair_s.at[0], recv_sem=pair_r.at[0],
        device_id=core, device_id_type=MESH,
    )
    swap.start()
    count, half_d = tok.shape[1], tok.shape[2]

    if inside:
        head = Gather(place, headb, head_sems)
        loads[3].wait()
        head.start()
    if inside:
        loads[4].wait()
        lend = pltpu.make_async_remote_copy(
            src_ref=cot.at[0], dst_ref=cot.at[1], send_sem=pair_s.at[2], recv_sem=pair_r.at[2],
            device_id=dev(z, 1 - x), device_id_type=MESH,
        )
        lend.start()

    def walk_old(s, carry):
        for part in old:
            part.step(s)
        if inside:
            head.step(s)
        return carry

    lax.fori_loop(1, nz + 1, walk_old, 0)
    for part in old:
        part.finish()
    loads[2].wait()
    feats = oldb.shape[2]

    slab = width.shape[0] // grown_parts
    for i, part in enumerate(grown):
        rows = pl.ds(i * slab, slab)

        @pl.loop(0, feats // 256)
        def _(j):
            cols = pl.ds(pl.multiple_of(j * 256, 256), 256)
            rhs = oldb[:, :, cols].reshape(-1, 256)
            grownb[g, rows, cols] = jnp.dot(
                width[rows, :], rhs, preferred_element_type=F32
            ).astype(BF16)

        part.start()

    grown_out[...] = grownb[g]
    swap.wait()

    @pl.loop(0, count // 16)
    def _(i):
        rows = pl.ds(pl.multiple_of(i * 16, 16), 16)
        a, b = tok[0, rows, :].astype(F32), tok[1, rows, :].astype(F32)
        total = jnp.sum(a * a, axis=-1, keepdims=True) + jnp.sum(b * b, axis=-1, keepdims=True)
        inv = lax.rsqrt(total * (1.0 / (2 * half_d)) + 1e-05)
        normed[rows, pl.ds(0, half_d)] = (a * inv * gain[:, pl.ds(0, half_d)]).astype(BF16)
        normed[rows, pl.ds(half_d, half_d)] = (b * inv * gain[:, pl.ds(half_d, half_d)]).astype(BF16)

    def walk_grown(s, carry):
        for part in grown:
            part.step(s)
        return carry

    lax.fori_loop(1, nz + 1, walk_grown, 0)
    for part in grown:
        part.finish()

    @pl.loop(0, feats // 256)
    def _(j):
        cols = pl.ds(pl.multiple_of(j * 256, 256), 256)
        rhs = grownb[:, :, cols].reshape(-1, 256)
        mixed[c, :, cols] = jnp.dot(normed[...], rhs, preferred_element_type=F32).astype(BF16)

    share = pltpu.make_async_remote_copy(
        src_ref=mixed.at[c], dst_ref=mixed.at[c], send_sem=pair_s.at[1], recv_sem=pair_r.at[1],
        device_id=core, device_id_type=MESH,
    )
    share.start()
    share.wait()

    if inside:
        w = headb.shape[2]
        per_half = n // 2

        def block(slot):
            cols = pl.ds(pl.multiple_of((slot % per_half) * w, w), w)
            return mixed.at[slot // per_half, :, cols]

        def hand(k):
            return pltpu.make_async_remote_copy(
                src_ref=block(k * 2 + 1 - x), dst_ref=theirs.at[k], send_sem=xs.at[k],
                recv_sem=xr.at[k], device_id=dev(z, 1 - x), device_id_type=MESH,
            )

        def offer(i, carry):
            @pl.when(nz - 1 - i > i)
            def _():
                hand(nz - 1 - i).start()

            @pl.when(nz - 1 - i >= i)
            def _():
                hand(i).start()
            return carry

        lax.fori_loop(0, nz, offer, 0)
        lend.wait_recv()

        def partial(k):
            rows = (((0,), (0,)), ((), ()))
            mine = lax.dot_general(block(k * 2 + x)[...], cot[0], rows, preferred_element_type=F32)
            return mine + lax.dot_general(theirs[k], cot[1], rows, preferred_element_type=F32)

        def rise(k):
            return pltpu.make_async_remote_copy(
                src_ref=tz.at[k], dst_ref=ru.at[k], send_sem=zs.at[k], recv_sem=ur.at[k],
                device_id=dev(z + 1, x), device_id_type=MESH,
            )

        def sink(k):
            return pltpu.make_async_remote_copy(
                src_ref=tz.at[k], dst_ref=rd.at[k], send_sem=zs.at[k], recv_sem=dr.at[k],
                device_id=dev(z - 1, x), device_id_type=MESH,
            )

        def mine(k, carry):
            hand(k).wait_recv()
            return carry

        lax.fori_loop(0, nz, mine, 0)

        def chain(i, carry):
            k = nz - 1 - i

            @pl.when(k > z)
            def _():
                own[...] = partial(k)

                @pl.when(z > 0)
                def _():
                    rise(k).wait_recv()
                    own[...] += ru[k].astype(F32)

                tz[k] = own[...].astype(BF16)
                rise(k).start()

            @pl.when(i < z)
            def _():
                own[...] = partial(i)

                @pl.when(z < nz - 1)
                def _():
                    sink(i).wait_recv()
                    own[...] += rd[i].astype(F32)

                tz[i] = own[...].astype(BF16)
                sink(i).start()
            return carry

        lax.fori_loop(0, nz - 1, chain, 0)
        own[...] = partial(z)
        head.finish()

        @pl.loop(0, value_out.shape[1] // 256)
        def _(j):
            outs = pl.ds(pl.multiple_of(j * 256, 256), 256)
            total = jnp.zeros((count, 256), F32)
            for slot in range(n):
                lhs = mixed[slot // per_half, :, pl.ds((slot % per_half) * w, w)]
                total = total + lax.dot_general(
                    lhs, headb[slot, outs, :], (((1,), (1,)), ((), ())), preferred_element_type=F32
                )
            value_out[:, outs] = total.astype(BF16)

        @pl.when(z > 0)
        def _():
            rise(z).wait_recv()
            own[...] += ru[z].astype(F32)

        @pl.when(z < nz - 1)
        def _():
            sink(z).wait_recv()
            own[...] += rd[z].astype(F32)

        grad_out[...] = own[...] * scale
        lend.wait_send()

        def sent(k, carry):
            hand(k).wait_send()

            @pl.when(k > z)
            def _():
                rise(k).wait_send()

            @pl.when(k < z)
            def _():
                sink(k).wait_send()
            return carry

        lax.fori_loop(0, nz, sent, 0)
        head.drain()
    else:
        mixed_out[...] = mixed[...]
    for part in old + grown:
        part.drain()


def cuts(rows):
    return 2 if rows % 256 == 0 else 1


def gather_sems(n):
    dma = pltpu.SemaphoreType.DMA
    return [dma((n,)), dma((n,)), dma((n // 2,)), dma((n // 2,)), dma((n // 2,)), dma((n,))]


def per_device(tokens, norm_gain, grow_width, old_value, grow_head, cotangent):
    n = lax.axis_size("fsdp")
    count, half_d = tokens.shape
    feats = old_value.shape[1]
    slab = grow_width.shape[0]
    heads, w = grow_head.shape
    inside = w % 128 == 0
    scale = 1.0 / math.sqrt(count * n)
    dma = pltpu.SemaphoreType.DMA
    vm = pl.BlockSpec(memory_space=pltpu.VMEM)
    hbm = pl.BlockSpec(memory_space=pl.ANY)
    outs = [jax.ShapeDtypeStruct((slab, feats), BF16)]
    if inside:
        outs += [jax.ShapeDtypeStruct((count, heads), BF16), jax.ShapeDtypeStruct((w, heads), F32)]
    else:
        outs += [jax.ShapeDtypeStruct((2, count, feats), BF16)]
    scratch = [
        pltpu.VMEM((2, count, half_d), BF16),
        pltpu.VMEM(grow_width.shape, BF16),
        pltpu.VMEM((count, 2 * half_d), BF16),
        pltpu.VMEM((2, count, feats), BF16),
        pltpu.VMEM((n,) + old_value.shape, BF16),
        pltpu.VMEM((n, slab, feats), BF16),
        *(gather_sems(n) * cuts(old_value.shape[0])), *(gather_sems(n) * cuts(slab)),
        dma((5,)), dma((3,)), dma((3,)),
    ]
    if inside:
        piece = pltpu.VMEM((n // 2, w, heads), BF16)
        scratch += [
            pltpu.VMEM((n, heads, w), BF16), pltpu.VMEM((2, count, heads), BF16),
            pltpu.VMEM((n // 2, count, w), BF16), piece, piece, piece, pltpu.VMEM((w, heads), F32),
            *gather_sems(n),
            dma((n // 2,)), dma((n // 2,)), dma((n // 2,)), dma((n // 2,)), dma((n // 2,)),
        ]
    results = pl.pallas_call(
        functools.partial(kernel, n, inside, scale),
        out_shape=outs,
        in_specs=[hbm, vm, hbm, hbm, hbm, hbm],
        out_specs=[vm] * len(outs),
        scratch_shapes=scratch,
        compiler_params=pltpu.CompilerParams(
            collective_id=0, has_side_effects=True, vmem_limit_bytes=48 * 1024 * 1024
        ),
    )(tokens, norm_gain.reshape(1, -1), grow_width, old_value, grow_head, cotangent)
    if inside:
        return tuple(results)
    grown_value, halves = results
    mixed = jnp.concatenate([halves[0], halves[1]], axis=1)
    head_all = lax.all_gather(grow_head, "fsdp", axis=1, tiled=True)
    value_out = lax.dot_general(
        mixed, head_all, (((1,), (1,)), ((), ())), preferred_element_type=F32
    ).astype(BF16)
    partial = lax.dot_general(
        mixed, cotangent, (((0,), (0,)), ((), ())), preferred_element_type=F32
    ).astype(BF16)
    partial = partial.reshape(n, partial.shape[0] // n, partial.shape[1])
    parts = lax.all_to_all(partial, "fsdp", split_axis=0, concat_axis=0, tiled=True)
    return (grown_value, value_out, jnp.sum(parts.astype(F32), axis=0) * scale)


def solution(mesh):
    return jax.shard_map(
        per_device,
        mesh=mesh,
        in_specs=(
            P(("trial", "fsdp"), "tensor"),
            P(),
            P("fsdp", None),
            P("fsdp", "tensor"),
            P("tensor", "fsdp"),
            P(("trial", "fsdp"), "tensor"),
        ),
        out_specs=(
            P(("trial", "fsdp"), "tensor"),
            P(("trial", "fsdp"), "tensor"),
            P(("trial", "fsdp"), "tensor"),
        ),
        check_vma=False,
    )
```
